32 devices in a mesh: row: 16 (over z, x, core), col: 2 (over y).
Axes of the slice: x: 2, y: 2, z: 4, core: 2. Of those that a mesh axis runs over, the one named last changes fastest.
Arguments:
- embeddings: bfloat16 [16384, 768], P(('row', 'col')), may hold values from -7.5 to 7.5
- block_cluster: int32 [64], replicated, may hold values from 0 to 15, never falling along the last dimension, each value on 1 to 8 neighbouring positions
- partner_shift: int32 [16384], P(('row', 'col')), may hold values from 1 to 255
Outputs:
- item_loss: float32 [16384], P(('row', 'col'))
- embedding_grad: float32 [16384, 768], P(('row', 'col'))
The draws below stay inside these ranges and needn't reach their ends.
Inputs may be any that keep to these rules, and one draw needn't show every extreme that they name: block_cluster never falls along the blocks; each value is held by 1 to 8 consecutive blocks, and some value by exactly 8.
All inputs are finite; a program needn't handle non-finite values.
Results may differ from the reference program's by a relative error of at most 0.0018.
Values may be sent and summed in bfloat16 or wider, within the bound.
A program may use at most 128 MiB of HBM per device.

```python
import math
import jax
import jax.numpy as jnp
import numpy as np
from jax import lax

D = 768
BLOCK = 256
MOST = 8
ITEMS = 16384
BLOCKS = 64
CLUSTERS = 16


def draw_embeddings(key, part):
    k_base, k_scale = jax.random.split(key, 2)
    base = jax.random.normal(k_base, (ITEMS, D), jnp.float32)
    spread = jax.random.uniform(k_scale, (ITEMS, 1), jnp.float32, math.log(0.5), math.log(2.0))
    values = jnp.clip(base * jnp.exp(spread), -7.5, 7.5)
    return values.astype(jnp.bfloat16)


def plant(entries, own_key, least, high):
    longest = entries.shape.index(max(entries.shape))
    spots = []
    for shift in (0, 1):
        where = [jax.random.randint(jax.random.fold_in(own_key, axis), (), 0, length) for axis, length in enumerate(entries.shape)]
        where[longest] = (where[longest] + shift) % entries.shape[longest]
        spots.append(tuple(where))
    return entries.at[spots[0]].set(least).at[spots[1]].set(high)


def length_profile(number_of, total, limit, lean):
    loads = [(1 << 20) // math.isqrt(standing ** lean) + 1 for standing in range(2, number_of + 1)]
    rest, given = total - limit - (number_of - 1), [1] * (number_of - 1)
    while rest > 0:
        movable = [i for i in range(number_of - 1) if given[i] < limit]
        whole, remaining = sum([loads[i] for i in movable]), rest
        for i in movable:
            extra = min(limit - given[i], max(1, remaining * loads[i] // whole), rest)
            given[i] = given[i] + extra
            rest = rest - extra
    return np.array([limit] + given)


def uneven_parts(stream_key, number_of, total, most, slope):
    if number_of == 2:
        one = jax.random.randint(stream_key, (), max(1, total - most), min(most, total - 1) + 1)
        return jnp.stack([one, total - one])
    sizes = jnp.asarray(length_profile(number_of, total, most, slope), jnp.int32)
    couples = (number_of - 1) // 2
    giver, taker = sizes[1:1 + 2 * couples:2], sizes[2:2 + 2 * couples:2]
    room = jnp.minimum(giver - 1, most - taker)
    moved = jax.random.randint(jax.random.fold_in(stream_key, 1), (couples,), 0, 1 << 20) % (room + 1)
    sizes = sizes.at[1:1 + 2 * couples:2].set(giver - moved).at[2:2 + 2 * couples:2].set(taker + moved)
    return sizes[jax.random.permutation(jax.random.fold_in(stream_key, 2), number_of)]


def setup_inputs(seed: int = 0) -> dict:
    key_list = jax.random.split(jax.random.key(seed), 4)
    embeddings = draw_embeddings(jax.random.fold_in(key_list[3], 71), 0)
    block_cluster = jnp.searchsorted(jnp.cumsum(uneven_parts(key_list[1], CLUSTERS, BLOCKS, MOST, 2)), jnp.arange(BLOCKS), side="right").astype(jnp.int32)
    partner_shift = plant(jax.random.randint(key_list[2], (ITEMS,), 1, BLOCK), jax.random.fold_in(key_list[2], 1), 1, BLOCK - 1).astype(jnp.int32)
    return {"embeddings": embeddings, "block_cluster": block_cluster, "partner_shift": partner_shift}


NEG = -1.0e30


def shift_blocks(values, offset):
    if offset == 0:
        return values
    pad = jnp.zeros((abs(offset),) + values.shape[1:], values.dtype)
    if offset > 0:
        return jnp.concatenate([values[offset:], pad], 0)
    return jnp.concatenate([pad, values[:offset]], 0)


def reference(embeddings, block_cluster, partner_shift):
    nblocks = ITEMS // BLOCK
    scale = D ** -0.5
    span = MOST - 1
    blocked = embeddings.astype(jnp.float32).reshape(nblocks, BLOCK, D)
    index = jnp.arange(nblocks, dtype=jnp.int32)
    position = jnp.arange(BLOCK, dtype=jnp.int32)
    diagonal = position[:, None] == position[None, :]

    def live_at(offset):
        valid = (index + offset >= 0) & (index + offset < nblocks)
        same = block_cluster == shift_blocks(block_cluster, offset)
        live = jnp.broadcast_to((valid & same)[:, None, None], (nblocks, BLOCK, BLOCK))
        if offset == 0:
            live = live & jnp.logical_not(diagonal)[None]
        return live

    def scores_at(offset):
        partner = shift_blocks(blocked, offset)
        return jnp.einsum("abd,acd->abc", blocked, partner, precision=lax.Precision.HIGHEST) * scale

    top = jnp.full((nblocks, BLOCK), NEG, jnp.float32)
    total = jnp.zeros((nblocks, BLOCK), jnp.float32)
    for offset in range(-span, span + 1):
        live = live_at(offset)
        masked = jnp.where(live, scores_at(offset), NEG)
        new_top = jnp.maximum(top, jnp.max(masked, axis=2))
        total = total * jnp.exp(top - new_top) + jnp.sum(jnp.where(live, jnp.exp(masked - new_top[:, :, None]), 0.0), axis=2)
        top = new_top
    lse = top + jnp.log(total)

    shifts = partner_shift.reshape(nblocks, BLOCK)
    partner = (position[None, :] + shifts) % BLOCK
    positive = position[None, None, :] == partner[:, :, None]
    self_scores = scores_at(0)
    loss = lse - jnp.sum(jnp.where(positive, self_scores, 0.0), axis=2)

    grad = jnp.zeros((nblocks, BLOCK, D), jnp.float32)
    for offset in range(-span, span + 1):
        live = live_at(offset)
        scores = scores_at(offset)
        rowwise = jnp.exp(jnp.where(live, scores - lse[:, :, None], NEG))
        if offset == 0:
            rowwise = rowwise - positive.astype(jnp.float32)
            both = rowwise + jnp.swapaxes(rowwise, 1, 2)
        else:
            far = shift_blocks(lse, offset)
            both = rowwise + jnp.exp(jnp.where(live, scores - far[:, None, :], NEG))
        weights = lax.optimization_barrier(both.astype(jnp.bfloat16)).astype(jnp.float32)
        grad = grad + jnp.einsum("abc,acd->abd", weights, shift_blocks(blocked, offset), precision=lax.Precision.HIGHEST) * scale
    return loss.reshape(ITEMS), grad.reshape(ITEMS, D)
```

```python
import functools

import jax
import jax.numpy as jnp
from jax import lax
from jax.experimental import pallas as pl
from jax.experimental.pallas import tpu as pltpu
from jax.sharding import PartitionSpec as P

BLOCK = 256
REACH = 4
CHUNK = 128
NEG = -1e30
F32 = jnp.float32


def kernel(
    row_axis, col_axis, devices, cols, scale,
    live_ref, e_ref, qcol_ref, qrow_ref,
    grad_ref, loss_ref,
    buf, scores, weights, top, total, lse_col, lse_send, lse_far, pos_score,
    recv, xs, ys, cs, zs, ls, lr,
):
    me = lax.axis_index(row_axis) * cols + lax.axis_index(col_axis)
    y = me % 2
    c = me // 2 % 2
    x = me // 4 % 2
    g = 2 * c + y
    gy = 2 * c + 1 - y
    gp = 2 * (1 - c) + y
    gpy = 2 * (1 - c) + 1 - y
    oth = 32 * (1 - x)
    adj = 32 * x
    xpeer = me + 4 - 8 * x
    ypeer = me + 1 - 2 * y
    cpeer = me + 2 - 4 * c
    zto = me + 8 - 16 * x
    zfrom = me - 8 + 16 * x
    z_send = (zto >= 0) & (zto < devices)
    z_recv = (zfrom >= 0) & (zfrom < devices)

    def at(device):
        return (device // cols, device % cols)

    def exists(device):
        return (device >= 0) & (device < devices)

    barrier = pltpu.get_barrier_semaphore()
    count = jnp.int32(0)
    for offset in (-8, -4, -3, -2, -1, 1, 2, 3, 4, 8):
        there = exists(me + offset)
        count = count + there.astype(jnp.int32)

        @pl.when(there)
        def _():
            pl.semaphore_signal(
                barrier, inc=1, device_id=at(me + offset), device_id_type=pl.DeviceIdType.MESH
            )
    pl.semaphore_wait(barrier, count)

    def rows(slot):
        return buf.at[pl.ds(pl.multiple_of(slot * CHUNK, CHUNK), CHUNK), :]

    def remote(src, slot, send, device):
        return pltpu.make_async_remote_copy(
            src_ref=src, dst_ref=rows(slot), send_sem=send, recv_sem=recv.at[slot],
            device_id=at(device), device_id_type=pl.DeviceIdType.MESH,
        )

    def own(i):
        return e_ref.at[pl.ds(i * CHUNK, CHUNK), :]

    def x_own(i):
        return remote(own(i), adj + 4 * g + i, xs.at[i], xpeer)

    def y_own(i):
        return remote(own(i), 16 + 4 * g + i, ys.at[i], ypeer)

    def c_own(i):
        return remote(own(i), 16 + 4 * g + i, cs.at[16 + 4 * g + i], cpeer)

    def x_relay(i):
        return remote(rows(16 + 4 * gy + i), adj + 4 * gy + i, xs.at[4 + i], xpeer)

    def y_relay(i):
        return remote(rows(oth + 4 * g + i), oth + 4 * g + i, ys.at[2 + i], ypeer)

    def z_need(r):
        return jnp.where(x == 0, r >= 4 * y + 2, r <= 4 * y + 9)

    def z_relay(r):
        return remote(rows(oth + r), adj + r, zs.at[r], zto)

    def c_relay(slot):
        return remote(rows(slot), slot, cs.at[slot], cpeer)

    def c_gives(slot):
        return (slot >= 4 * gp + 2) & (slot <= 4 * gp + 33)

    def c_takes(slot):
        return (slot >= 4 * g + 2) & (slot <= 4 * g + 33)

    def arrived(slot):
        remote(rows(slot), slot, zs.at[0], cpeer).wait_recv()

    def when(cond, action):
        pl.when(cond)(action)

    for i in range(4):
        x_own(i).start()
        y_own(i).start()
        c_own(i).start()

    when(~z_recv, lambda: buf.__setitem__(
        (pl.ds(pl.multiple_of(adj * CHUNK, CHUNK), 16 * CHUNK), slice(None)),
        jnp.zeros((16 * CHUNK, buf.shape[1]), buf.dtype)))
    for offset in (-4, -3, -2, -1, 1, 2, 3, 4):
        when(~exists(me + offset), lambda: lse_far.__setitem__(
            offset + 4, jnp.zeros(lse_far.shape[1:], F32)))

    n = e_ref.shape[0]

    half = lax.broadcasted_iota(jnp.int32, (n, BLOCK), 0)
    lane = lax.broadcasted_iota(jnp.int32, (n, BLOCK), 1)
    q = qcol_ref[...]
    own_scores = []
    for h in range(2):
        s = lax.dot_general(
            e_ref[...], e_ref[h * BLOCK:(h + 1) * BLOCK, :], (((1,), (1,)), ((), ())),
            preferred_element_type=F32) * scale
        cell = lane + h * BLOCK
        hit = jnp.sum(jnp.where(q == cell, s, 0.0), axis=1, keepdims=True)
        own_scores.append((s, hit))
        ok = jnp.concatenate(
            [jnp.full((BLOCK, BLOCK), live_ref[7 + h, r], jnp.int32) for r in range(2)], 0) > 0
        scores[7 + h] = jnp.where(ok & (half != cell), s, NEG)
    buf[pl.ds(pl.multiple_of((16 + 4 * g) * CHUNK, 4 * CHUNK), n), :] = e_ref[...]
    pos_score[...] = own_scores[0][1] + own_scores[1][1]
    m = jnp.maximum(jnp.max(scores[7], axis=1, keepdims=True), jnp.max(scores[8], axis=1, keepdims=True))
    top[...] = m
    total[...] = jnp.sum(jnp.exp(scores[7] - m), axis=1, keepdims=True) + jnp.sum(
        jnp.exp(scores[8] - m), axis=1, keepdims=True)

    def process(block):
        k = block - (2 * g + 1)

        @pl.when((k >= 0) & (k < 16))
        def _():
            far = buf[pl.ds(pl.multiple_of(block * BLOCK, BLOCK), BLOCK), :]
            for r in range(2):
                part = pl.ds(r * BLOCK, BLOCK)
                s = lax.dot_general(
                    e_ref[part, :], far, (((1,), (1,)), ((), ())),
                    preferred_element_type=F32) * scale
                s = jnp.where(live_ref[k, r] > 0, s, NEG)
                scores[k, part, :] = s
                old = top[part, :]
                new = jnp.maximum(old, jnp.max(s, axis=1, keepdims=True))
                total[part, :] = total[part, :] * jnp.exp(old - new) + jnp.sum(
                    jnp.exp(s - new), axis=1, keepdims=True)
                top[part, :] = new

    def give(slot, also=True):
        when(c_gives(slot) & also, lambda: c_relay(slot).start())

    def event(kind, i):
        if kind == "X":
            slot = oth + 4 * g + i
            arrived(slot)
            when(z_send & z_need(4 * g + i), lambda: z_relay(4 * g + i).start())
            if i >= 2:
                y_relay(i).start()
            give(slot)
        elif kind == "Y":
            slot = 16 + 4 * gy + i
            arrived(slot)
            if i < 2:
                x_relay(i).start()
            give(slot)
        elif kind == "D":
            slot = oth + 4 * gy + i
            arrived(slot)
            when(z_send & z_need(4 * gy + i), lambda: z_relay(4 * gy + i).start())
            give(slot)
        else:
            e = 4 * (g if kind == "Z" else gy) + i

            def take():
                arrived(adj + e)
                give(adj + e)
            when(z_recv & z_need(e), take)

    def c_wait(base, cond=True):
        for i in range(4):
            when(c_takes(base + i) & cond, lambda: arrived(base + i))

    steps = [
        ([("X", 0), ("Y", 0), ("X", 1), ("Y", 1)], (16 + 4 * gp, "own"), 16 + 4 * gp),
        ([("X", 2), ("Y", 2), ("Z", 0), ("X", 3), ("Y", 3), ("Z", 1)], None, oth + 4 * g),
        ([], None, 16 + 4 * gy),
        ([("D", 0), ("D", 2), ("Z", 2)], (16 + 4 * gpy, True), 16 + 4 * gpy),
        ([("D", 1), ("D", 3), ("Z", 3)], (oth + 4 * gp, True), oth + 4 * gp),
        ([], None, oth + 4 * gy),
        ([("W", 0), ("W", 2)], (oth + 4 * gpy, True), oth + 4 * gpy),
        ([("W", 1), ("W", 3)], None, adj + 4 * g),
        ([], (adj + 4 * gp, z_recv), adj + 4 * gp),
        ([], None, adj + 4 * gy),
        ([], (adj + 4 * gpy, z_recv), adj + 4 * gpy),
    ]

    def step(u, carry):
        base = jnp.int32(0)
        for index, (events, cwait, slot) in enumerate(steps):
            base = base + jnp.where(u == index, slot, 0)
            if events or cwait is not None:
                @pl.when(u == index)
                def _():
                    for kind, i in events:
                        event(kind, i)
                    if cwait is not None:
                        if cwait[1] == "own":
                            for i in range(4):
                                arrived(cwait[0] + i)
                        else:
                            c_wait(*cwait)
        for h in range(2):
            process(base // 2 + h)
        return carry

    lax.fori_loop(0, len(steps), step, 0)

    lse = top[...] + jnp.log(total[...])
    lse_col[...] = lse
    loss = lse - pos_score[...]
    both = jnp.where(
        lax.broadcasted_iota(jnp.int32, (n, 128), 1) < 8,
        jnp.broadcast_to(lse, (n, 128)), jnp.broadcast_to(loss, (n, 128)))
    turned = both.T
    lse_send[...] = turned[:8, :]
    lse_far[4] = turned[:8, :]
    loss_ref[...] = turned[8:9, :]

    def lse_copy(offset):
        return pltpu.make_async_remote_copy(
            src_ref=lse_send, dst_ref=lse_far.at[4 - offset],
            send_sem=ls.at[4 + offset], recv_sem=lr.at[4 - offset],
            device_id=at(me + offset), device_id_type=pl.DeviceIdType.MESH,
        )

    for offset in (-4, 4, -3, 3, -2, 2, -1, 1):
        when(exists(me + offset), lambda: lse_copy(offset).start())

    def fill(k):
        offset = (k - 7) // 2
        h = (k - 7) % 2
        s = scores[k]
        w = jnp.exp(s - lse_col[...]) + jnp.exp(
            s - lse_far[offset + 4][0:1, h * BLOCK:(h + 1) * BLOCK])
        if offset == 0:
            cell = lax.broadcasted_iota(jnp.int32, (n, BLOCK), 1) + h * BLOCK
            line = lax.broadcasted_iota(jnp.int32, (n, BLOCK), 0)
            w = w - (qcol_ref[...] == cell).astype(F32)
            w = w - (qrow_ref[0:1, h * BLOCK:(h + 1) * BLOCK] == line).astype(F32)
        weights[:, k * BLOCK:(k + 1) * BLOCK] = w.astype(jnp.bfloat16)

    fill(7)
    fill(8)
    for offset in (-1, 1, -2, 2, -3, 3, -4, 4):
        when(exists(me + offset), lambda: lse_copy(-offset).wait_recv())
        for k in range(16):
            if (k - 7) // 2 == offset:
                fill(k)

    width = e_ref.shape[1]

    def product(t, carry):
        columns = pl.ds(pl.multiple_of(t * 256, 256), 256)
        near = buf[pl.ds(pl.multiple_of((2 * g + 1) * BLOCK, BLOCK), 16 * BLOCK), columns]
        grad_ref[:, columns] = jnp.dot(weights[...], near, preferred_element_type=F32) * scale
        return carry

    lax.fori_loop(0, width // 256, product, 0)

    for offset in (-4, 4, -3, 3, -2, 2, -1, 1):
        when(exists(me + offset), lambda: lse_copy(offset).wait_send())
    for i in range(4):
        x_own(i).wait_send()
        y_own(i).wait_send()
        c_own(i).wait_send()
        when(z_send & z_need(4 * g + i), lambda: z_relay(4 * g + i).wait_send())
        when(z_send & z_need(4 * gy + i), lambda: z_relay(4 * gy + i).wait_send())
        for slot in (oth + 4 * g + i, 16 + 4 * gy + i, oth + 4 * gy + i):
            when(c_gives(slot), lambda: c_relay(slot).wait_send())
        for e in (4 * g + i, 4 * gy + i):
            when(c_gives(adj + e) & z_recv & z_need(e), lambda: c_relay(adj + e).wait_send())
        if i < 2:
            x_relay(i).wait_send()
        else:
            y_relay(i).wait_send()


def solution(mesh):
    row_axis, col_axis = mesh.axis_names
    devices = mesh.shape[row_axis] * mesh.shape[col_axis]
    cols = mesh.shape[col_axis]

    def shards(embeddings, block_cluster, partner_shift):
        rows, width = embeddings.shape
        blocks = rows // BLOCK
        device = lax.axis_index((row_axis, col_axis))
        margin = jnp.full((7,), -1, jnp.int32)
        beyond = jnp.full((8,), -2, jnp.int32)
        padded = jnp.concatenate([margin, block_cluster, beyond])
        window = lax.dynamic_slice_in_dim(padded, device * blocks, 16)
        live = (window[:, None] == window[None, 7:9]).astype(jnp.int32)
        position = jnp.arange(rows, dtype=jnp.int32)
        within = position % BLOCK
        partner = position - within + (within + partner_shift) % BLOCK
        vmem = pl.BlockSpec(memory_space=pltpu.VMEM)
        grad, loss = pl.pallas_call(
            functools.partial(kernel, row_axis, col_axis, devices, cols, width ** (-0.5)),
            out_shape=(
                jax.ShapeDtypeStruct((rows, width), F32),
                jax.ShapeDtypeStruct((1, rows), F32),
            ),
            in_specs=[pl.BlockSpec(memory_space=pltpu.SMEM), vmem, vmem, vmem],
            out_specs=(vmem, vmem),
            scratch_shapes=[
                pltpu.VMEM((24 * BLOCK, width), jnp.bfloat16),
                pltpu.VMEM((16, rows, BLOCK), F32),
                pltpu.VMEM((rows, 16 * BLOCK), jnp.bfloat16),
                pltpu.VMEM((rows, 1), F32),
                pltpu.VMEM((rows, 1), F32),
                pltpu.VMEM((rows, 1), F32),
                pltpu.VMEM((8, rows), F32),
                pltpu.VMEM((2 * REACH + 1, 8, rows), F32),
                pltpu.VMEM((rows, 1), F32),
                pltpu.SemaphoreType.DMA((48,)),
                pltpu.SemaphoreType.DMA((6,)),
                pltpu.SemaphoreType.DMA((6,)),
                pltpu.SemaphoreType.DMA((48,)),
                pltpu.SemaphoreType.DMA((16,)),
                pltpu.SemaphoreType.DMA((2 * REACH + 1,)),
                pltpu.SemaphoreType.DMA((2 * REACH + 1,)),
            ],
            compiler_params=pltpu.CompilerParams(
                collective_id=0, has_side_effects=True, vmem_limit_bytes=60 * 1024 * 1024
            ),
        )(live, embeddings, partner[:, None], partner[None, :])
        return loss.reshape(rows), grad

    in_specs = (P((row_axis, col_axis), None), P(), P((row_axis, col_axis)))
    out_specs = (P((row_axis, col_axis)), P((row_axis, col_axis), None))
    return jax.shard_map(shards, mesh=mesh, in_specs=in_specs, out_specs=out_specs, check_vma=False)
```

```python
import functools

import jax
import jax.numpy as jnp
from jax import lax
from jax.experimental import pallas as pl
from jax.experimental.pallas import tpu as pltpu
from jax.sharding import PartitionSpec as P

BLOCK = 256
REACH = 4
CHUNK = 128
NEG = -1e30
F32 = jnp.float32


def kernel(
    row_axis, col_axis, devices, cols, scale,
    cluster_ref, e_ref, shift_ref,
    grad_ref, loss_ref,
    buf, scores, weights, top, total, lse_col, lse_send, lse_far, pos_score, qcol_ref, qrow_ref,
    recv, xs, ys, cs, zs, ls, lr,
):
    me = lax.axis_index(row_axis) * cols + lax.axis_index(col_axis)
    y = me % 2
    c = me // 2 % 2
    x = me // 4 % 2
    g = 2 * c + y
    gy = 2 * c + 1 - y
    gp = 2 * (1 - c) + y
    gpy = 2 * (1 - c) + 1 - y
    oth = 32 * (1 - x)
    adj = 32 * x
    xpeer = me + 4 - 8 * x
    ypeer = me + 1 - 2 * y
    cpeer = me + 2 - 4 * c
    zto = me + 8 - 16 * x
    zfrom = me - 8 + 16 * x
    z_send = (zto >= 0) & (zto < devices)
    z_recv = (zfrom >= 0) & (zfrom < devices)

    def at(device):
        return (device // cols, device % cols)

    def exists(device):
        return (device >= 0) & (device < devices)

    barrier = pltpu.get_barrier_semaphore()
    count = jnp.int32(0)
    for offset in (-8, -4, -3, -2, -1, 1, 2, 3, 4, 8):
        there = exists(me + offset)
        count = count + there.astype(jnp.int32)

        @pl.when(there)
        def _():
            pl.semaphore_signal(
                barrier, inc=1, device_id=at(me + offset), device_id_type=pl.DeviceIdType.MESH
            )
    pl.semaphore_wait(barrier, count)

    def rows(slot):
        return buf.at[pl.ds(pl.multiple_of(slot * CHUNK, CHUNK), CHUNK), :]

    def remote(src, slot, send, device):
        return pltpu.make_async_remote_copy(
            src_ref=src, dst_ref=rows(slot), send_sem=send, recv_sem=recv.at[slot],
            device_id=at(device), device_id_type=pl.DeviceIdType.MESH,
        )

    def own(i):
        return e_ref.at[pl.ds(i * CHUNK, CHUNK), :]

    def x_own(i):
        return remote(own(i), adj + 4 * g + i, xs.at[i], xpeer)

    def y_own(i):
        return remote(own(i), 16 + 4 * g + i, ys.at[i], ypeer)

    def c_own(i):
        return remote(own(i), 16 + 4 * g + i, cs.at[16 + 4 * g + i], cpeer)

    def x_relay(i):
        return remote(rows(16 + 4 * gy + i), adj + 4 * gy + i, xs.at[4 + i], xpeer)

    def y_relay(i):
        return remote(rows(oth + 4 * g + i), oth + 4 * g + i, ys.at[2 + i], ypeer)

    def z_need(r):
        return jnp.where(x == 0, r >= 4 * y + 2, r <= 4 * y + 9)

    def z_relay(r):
        return remote(rows(oth + r), adj + r, zs.at[r], zto)

    zy_send = z_recv & (c == 0) & (y == 1 - x)
    zy_skip = (c == 0) & (y == x)

    def z_gives(i):
        need = z_send & z_need(4 * gy + i)
        return need & ~zy_skip if i >= 2 else need

    def zy_relay(i):
        return remote(rows(adj + 4 * g + i), adj + 4 * g + i, ys.at[4 + i], ypeer)

    def c_relay(slot):
        return remote(rows(slot), slot, cs.at[slot], cpeer)

    def c_gives(slot):
        return (slot >= 4 * gp + 2) & (slot <= 4 * gp + 33)

    def c_takes(slot):
        return (slot >= 4 * g + 2) & (slot <= 4 * g + 33)

    def arrived(slot):
        remote(rows(slot), slot, zs.at[0], cpeer).wait_recv()

    def when(cond, action):
        pl.when(cond)(action)

    for i in range(2):
        x_own(2 + i).start()
        y_own(i).start()
    for i in range(4):
        c_own(i).start()

    when(~z_recv, lambda: buf.__setitem__(
        (pl.ds(pl.multiple_of(adj * CHUNK, CHUNK), 16 * CHUNK), slice(None)),
        jnp.zeros((16 * CHUNK, buf.shape[1]), buf.dtype)))
    for offset in (-4, -3, -2, -1, 1, 2, 3, 4):
        when(~exists(me + offset), lambda: lse_far.__setitem__(
            offset + 4, jnp.zeros(lse_far.shape[1:], F32)))

    n = e_ref.shape[0]
    blocks = cluster_ref.shape[0]

    def alive(k, r):
        there = 2 * me + k - 7
        near = jnp.maximum(jnp.minimum(there, blocks - 1), 0)
        same = cluster_ref[near] == cluster_ref[2 * me + r]
        return same & (there == near)

    place = lax.broadcasted_iota(jnp.int32, (1, n), 1)
    within = place % BLOCK
    goal = place - within + (within + shift_ref[...]) % BLOCK
    qrow_ref[...] = goal
    qcol_ref[...] = jnp.broadcast_to(goal.astype(F32), (128, n)).T[:, :1].astype(jnp.int32)

    half = lax.broadcasted_iota(jnp.int32, (n, BLOCK), 0)
    lane = lax.broadcasted_iota(jnp.int32, (n, BLOCK), 1)
    q = qcol_ref[...]
    own_scores = []
    for h in range(2):
        s = lax.dot_general(
            e_ref[...], e_ref[h * BLOCK:(h + 1) * BLOCK, :], (((1,), (1,)), ((), ())),
            preferred_element_type=F32) * scale
        cell = lane + h * BLOCK
        hit = jnp.sum(jnp.where(q == cell, s, 0.0), axis=1, keepdims=True)
        own_scores.append((s, hit))
        ok = jnp.concatenate(
            [jnp.full((BLOCK, BLOCK), alive(7 + h, r).astype(jnp.int32), jnp.int32) for r in range(2)], 0) > 0
        scores[7 + h] = jnp.where(ok & (half != cell), s, NEG)
    buf[pl.ds(pl.multiple_of((16 + 4 * g) * CHUNK, 4 * CHUNK), n), :] = e_ref[...]
    pos_score[...] = own_scores[0][1] + own_scores[1][1]
    m = jnp.maximum(jnp.max(scores[7], axis=1, keepdims=True), jnp.max(scores[8], axis=1, keepdims=True))
    top[...] = m
    total[...] = jnp.sum(jnp.exp(scores[7] - m), axis=1, keepdims=True) + jnp.sum(
        jnp.exp(scores[8] - m), axis=1, keepdims=True)

    def process(block):
        k = block - (2 * g + 1)

        @pl.when((k >= 0) & (k < 16))
        def _():
            far = buf[pl.ds(pl.multiple_of(block * BLOCK, BLOCK), BLOCK), :]
            for r in range(2):
                part = pl.ds(r * BLOCK, BLOCK)
                s = lax.dot_general(
                    e_ref[part, :], far, (((1,), (1,)), ((), ())),
                    preferred_element_type=F32) * scale
                s = jnp.where(alive(k, r), s, NEG)
                scores[k, part, :] = s
                old = top[part, :]
                new = jnp.maximum(old, jnp.max(s, axis=1, keepdims=True))
                total[part, :] = total[part, :] * jnp.exp(old - new) + jnp.sum(
                    jnp.exp(s - new), axis=1, keepdims=True)
                top[part, :] = new

    def give(slot, also=True):
        when(c_gives(slot) & also, lambda: c_relay(slot).start())

    def event(kind, i):
        if kind == "X":
            slot = oth + 4 * g + i
            arrived(slot)
            when(z_send & z_need(4 * g + i), lambda: z_relay(4 * g + i).start())
            if i >= 2:
                y_relay(i).start()
                y_own(i).start()
            give(slot)
        elif kind == "Y":
            slot = 16 + 4 * gy + i
            arrived(slot)
            if i < 2:
                x_relay(i).start()
                x_own(i).start()
            give(slot)
        elif kind == "D":
            slot = oth + 4 * gy + i
            arrived(slot)
            when(z_gives(i), lambda: z_relay(4 * gy + i).start())
            give(slot)
        else:
            e = 4 * (g if kind == "Z" else gy) + i

            def take():
                arrived(adj + e)
                if kind == "Z" and i >= 2:
                    when(zy_send, lambda: zy_relay(i).start())
                give(adj + e)
            when(z_recv & z_need(e), take)

    def c_wait(block, cond):
        for i in range(2):
            when(c_takes(2 * block + i) & cond, lambda: arrived(2 * block + i))

    def at_block(base, element, h):
        return base // 2 + 2 * element + h

    here = jnp.int32(16)
    steps = [
        ([("X", 2), ("Y", 0)], [(at_block(here, gp, 0), True), (at_block(here, gp, 1), True)]),
        ([("X", 3), ("Y", 1), ("Z", 2)], [(at_block(oth, g, 1), None), (at_block(here, gy, 0), None)]),
        ([("D", 0), ("D", 2), ("Z", 3)], [(at_block(oth, gp, 1), True), (at_block(here, gpy, 0), True)]),
        ([("X", 0), ("Y", 2), ("W", 0)], [(at_block(adj, g, 1), None), (at_block(adj, gp, 1), z_recv)]),
        ([("D", 1), ("D", 3), ("W", 2)], [(at_block(oth, gy, 0), None), (at_block(oth, gy, 1), None)]),
        ([("X", 1), ("Y", 3), ("Z", 0)], [(at_block(oth, g, 0), None), (at_block(here, gy, 1), None)]),
        ([("W", 1)], [(at_block(oth, gp, 0), True), (at_block(here, gpy, 1), True)]),
        ([("W", 3)], [(at_block(oth, gpy, 0), True), (at_block(oth, gpy, 1), True)]),
        ([("Z", 1)], [(at_block(adj, gy, 0), None), (at_block(adj, gy, 1), None)]),
        ([], [(at_block(adj, gpy, 0), z_recv), (at_block(adj, gpy, 1), z_recv)]),
        ([], [(at_block(adj, g, 0), None), (at_block(adj, gp, 0), z_recv)]),
    ]

    def step(u, carry):
        spots = [jnp.int32(0), jnp.int32(0)]
        for index, (events, ready) in enumerate(steps):
            for h in range(2):
                spots[h] = spots[h] + jnp.where(u == index, ready[h][0], 0)

            @pl.when(u == index)
            def _():
                for kind, i in events:
                    event(kind, i)
                for block, cond in ready:
                    if cond is not None:
                        c_wait(block, cond)
        for h in range(2):
            process(spots[h])
        return carry

    lax.fori_loop(0, len(steps), step, 0)

    lse = top[...] + jnp.log(total[...])
    lse_col[...] = lse
    loss = lse - pos_score[...]
    both = jnp.where(
        lax.broadcasted_iota(jnp.int32, (n, 128), 1) < 8,
        jnp.broadcast_to(lse, (n, 128)), jnp.broadcast_to(loss, (n, 128)))
    turned = both.T
    lse_send[...] = turned[:8, :]
    lse_far[4] = turned[:8, :]
    loss_ref[...] = turned[8:9, :]

    def lse_copy(offset):
        return pltpu.make_async_remote_copy(
            src_ref=lse_send, dst_ref=lse_far.at[4 - offset],
            send_sem=ls.at[4 + offset], recv_sem=lr.at[4 - offset],
            device_id=at(me + offset), device_id_type=pl.DeviceIdType.MESH,
        )

    for offset in (-4, 4, -3, 3, -2, 2, -1, 1):
        when(exists(me + offset), lambda: lse_copy(offset).start())

    def fill(k):
        offset = (k - 7) // 2
        h = (k - 7) % 2
        s = scores[k]
        w = jnp.exp(s - lse_col[...]) + jnp.exp(
            s - lse_far[offset + 4][0:1, h * BLOCK:(h + 1) * BLOCK])
        if offset == 0:
            cell = lax.broadcasted_iota(jnp.int32, (n, BLOCK), 1) + h * BLOCK
            line = lax.broadcasted_iota(jnp.int32, (n, BLOCK), 0)
            w = w - (qcol_ref[...] == cell).astype(F32)
            w = w - (qrow_ref[0:1, h * BLOCK:(h + 1) * BLOCK] == line).astype(F32)
        weights[:, k * BLOCK:(k + 1) * BLOCK] = w.astype(jnp.bfloat16)

    fill(7)
    fill(8)
    for offset in (-1, 1, -2, 2, -3, 3, -4, 4):
        when(exists(me + offset), lambda: lse_copy(-offset).wait_recv())
        for k in range(16):
            if (k - 7) // 2 == offset:
                fill(k)

    width = e_ref.shape[1]

    def product(t, carry):
        columns = pl.ds(pl.multiple_of(t * 256, 256), 256)
        near = buf[pl.ds(pl.multiple_of((2 * g + 1) * BLOCK, BLOCK), 16 * BLOCK), columns]
        grad_ref[:, columns] = jnp.dot(weights[...], near, preferred_element_type=F32) * scale
        return carry

    lax.fori_loop(0, width // 256, product, 0)

    for offset in (-4, 4, -3, 3, -2, 2, -1, 1):
        when(exists(me + offset), lambda: lse_copy(offset).wait_send())
    for i in range(4):
        x_own(i).wait_send()
        y_own(i).wait_send()
        c_own(i).wait_send()
        when(z_send & z_need(4 * g + i), lambda: z_relay(4 * g + i).wait_send())
        when(z_gives(i), lambda: z_relay(4 * gy + i).wait_send())
        for slot in (oth + 4 * g + i, 16 + 4 * gy + i, oth + 4 * gy + i):
            when(c_gives(slot), lambda: c_relay(slot).wait_send())
        for e in (4 * g + i, 4 * gy + i):
            when(c_gives(adj + e) & z_recv & z_need(e), lambda: c_relay(adj + e).wait_send())
        if i < 2:
            x_relay(i).wait_send()
        else:
            y_relay(i).wait_send()
            when(zy_send, lambda: zy_relay(i).wait_send())


def solution(mesh):
    row_axis, col_axis = mesh.axis_names
    devices = mesh.shape[row_axis] * mesh.shape[col_axis]
    cols = mesh.shape[col_axis]

    def shards(embeddings, block_cluster, partner_shift):
        rows, width = embeddings.shape
        vmem = pl.BlockSpec(memory_space=pltpu.VMEM)
        grad, loss = pl.pallas_call(
            functools.partial(kernel, row_axis, col_axis, devices, cols, width ** (-0.5)),
            out_shape=(
                jax.ShapeDtypeStruct((rows, width), F32),
                jax.ShapeDtypeStruct((1, rows), F32),
            ),
            in_specs=[pl.BlockSpec(memory_space=pltpu.SMEM), vmem, vmem],
            out_specs=(vmem, vmem),
            scratch_shapes=[
                pltpu.VMEM((24 * BLOCK, width), jnp.bfloat16),
                pltpu.VMEM((16, rows, BLOCK), F32),
                pltpu.VMEM((rows, 16 * BLOCK), jnp.bfloat16),
                pltpu.VMEM((rows, 1), F32),
                pltpu.VMEM((rows, 1), F32),
                pltpu.VMEM((rows, 1), F32),
                pltpu.VMEM((8, rows), F32),
                pltpu.VMEM((2 * REACH + 1, 8, rows), F32),
                pltpu.VMEM((rows, 1), F32),
                pltpu.VMEM((rows, 1), jnp.int32),
                pltpu.VMEM((1, rows), jnp.int32),
                pltpu.SemaphoreType.DMA((48,)),
                pltpu.SemaphoreType.DMA((6,)),
                pltpu.SemaphoreType.DMA((8,)),
                pltpu.SemaphoreType.DMA((48,)),
                pltpu.SemaphoreType.DMA((16,)),
                pltpu.SemaphoreType.DMA((2 * REACH + 1,)),
                pltpu.SemaphoreType.DMA((2 * REACH + 1,)),
            ],
            compiler_params=pltpu.CompilerParams(
                collective_id=0, has_side_effects=True, vmem_limit_bytes=60 * 1024 * 1024
            ),
        )(block_cluster, embeddings, partner_shift.reshape(1, rows))
        return loss.reshape(rows), grad

    in_specs = (P((row_axis, col_axis), None), P(), P((row_axis, col_axis)))
    out_specs = (P((row_axis, col_axis)), P((row_axis, col_axis), None))
    return jax.shard_map(shards, mesh=mesh, in_specs=in_specs, out_specs=out_specs, check_vma=False)
```

```python
import functools

import jax
import jax.numpy as jnp
from jax import lax
from jax.experimental import pallas as pl
from jax.experimental.pallas import tpu as pltpu
from jax.sharding import PartitionSpec as P

BLOCK = 256
REACH = 4
CHUNK = 128
NEG = -1e30
F32 = jnp.float32


def kernel(
    row_axis, col_axis, devices, cols, scale,
    cluster_ref, e_ref, shift_ref,
    grad_ref, loss_ref,
    buf, scores, weights, top, total, lse_col, lse_send, lse_far, pos_score, qcol_ref, qrow_ref,
    recv, xs, ys, cs, zs, ls, lr,
):
    me = lax.axis_index(row_axis) * cols + lax.axis_index(col_axis)
    y = me % 2
    c = me // 2 % 2
    x = me // 4 % 2
    g = 2 * c + y
    gy = 2 * c + 1 - y
    gp = 2 * (1 - c) + y
    gpy = 2 * (1 - c) + 1 - y
    oth = 32 * (1 - x)
    adj = 32 * x
    xpeer = me + 4 - 8 * x
    ypeer = me + 1 - 2 * y
    cpeer = me + 2 - 4 * c
    zto = me + 8 - 16 * x
    zfrom = me - 8 + 16 * x
    z_send = (zto >= 0) & (zto < devices)
    z_recv = (zfrom >= 0) & (zfrom < devices)

    def at(device):
        return (device // cols, device % cols)

    def exists(device):
        return (device >= 0) & (device < devices)

    barrier = pltpu.get_barrier_semaphore()
    count = jnp.int32(0)
    for offset in (-8, -4, -3, -2, -1, 1, 2, 3, 4, 8):
        there = exists(me + offset)
        count = count + there.astype(jnp.int32)

        @pl.when(there)
        def _():
            pl.semaphore_signal(
                barrier, inc=1, device_id=at(me + offset), device_id_type=pl.DeviceIdType.MESH
            )
    pl.semaphore_wait(barrier, count)

    def rows(slot):
        return buf.at[pl.ds(pl.multiple_of(slot * CHUNK, CHUNK), CHUNK), :]

    def remote(src, slot, send, device):
        return pltpu.make_async_remote_copy(
            src_ref=src, dst_ref=rows(slot), send_sem=send, recv_sem=recv.at[slot],
            device_id=at(device), device_id_type=pl.DeviceIdType.MESH,
        )

    def own(i):
        return e_ref.at[pl.ds(i * CHUNK, CHUNK), :]

    def x_own(i):
        return remote(own(i), adj + 4 * g + i, xs.at[i], xpeer)

    def y_own(i):
        return remote(own(i), 16 + 4 * g + i, ys.at[i], ypeer)

    def c_own(i):
        return remote(own(i), 16 + 4 * g + i, cs.at[16 + 4 * g + i], cpeer)

    def x_relay(i):
        return remote(rows(16 + 4 * gy + i), adj + 4 * gy + i, xs.at[4 + i], xpeer)

    def y_relay(i):
        return remote(rows(oth + 4 * g + i), oth + 4 * g + i, ys.at[2 + i], ypeer)

    def z_need(r):
        return jnp.where(x == 0, r >= 4 * y + 2, r <= 4 * y + 9)

    def z_relay(r):
        return remote(rows(oth + r), adj + r, zs.at[r], zto)

    zy_send = z_recv & (c == 0) & (y == 1 - x)
    zy_skip = (c == 0) & (y == x)

    def z_gives(i):
        need = z_send & z_need(4 * gy + i)
        return need & ~zy_skip if i >= 2 else need

    def zy_relay(i):
        return remote(rows(adj + 4 * g + i), adj + 4 * g + i, ys.at[4 + i], ypeer)

    def c_relay(slot):
        return remote(rows(slot), slot, cs.at[slot], cpeer)

    def c_gives(slot):
        return (slot >= 4 * gp + 2) & (slot <= 4 * gp + 33)

    def c_takes(slot):
        return (slot >= 4 * g + 2) & (slot <= 4 * g + 33)

    def arrived(slot):
        remote(rows(slot), slot, zs.at[0], cpeer).wait_recv()

    def when(cond, action):
        pl.when(cond)(action)

    for i in range(2):
        x_own(2 + i).start()
        y_own(i).start()
    for i in range(4):
        c_own(i).start()

    when(~z_recv, lambda: buf.__setitem__(
        (pl.ds(pl.multiple_of(adj * CHUNK, CHUNK), 16 * CHUNK), slice(None)),
        jnp.zeros((16 * CHUNK, buf.shape[1]), buf.dtype)))
    for offset in (-4, -3, -2, -1, 1, 2, 3, 4):
        when(~exists(me + offset), lambda: lse_far.__setitem__(
            offset + 4, jnp.zeros(lse_far.shape[1:], F32)))

    n = e_ref.shape[0]
    blocks = cluster_ref.shape[0]

    def alive(k, r):
        there = 2 * me + k - 7
        near = jnp.maximum(jnp.minimum(there, blocks - 1), 0)
        same = cluster_ref[near] == cluster_ref[2 * me + r]
        return same & (there == near)

    place = lax.broadcasted_iota(jnp.int32, (1, n), 1)
    within = place % BLOCK
    goal = place - within + (within + shift_ref[...]) % BLOCK
    qrow_ref[...] = goal
    qcol_ref[...] = jnp.broadcast_to(goal.astype(F32), (128, n)).T[:, :1].astype(jnp.int32)

    half = lax.broadcasted_iota(jnp.int32, (n, BLOCK), 0)
    lane = lax.broadcasted_iota(jnp.int32, (n, BLOCK), 1)
    q = qcol_ref[...]
    own_scores = []
    for h in range(2):
        s = lax.dot_general(
            e_ref[...], e_ref[h * BLOCK:(h + 1) * BLOCK, :], (((1,), (1,)), ((), ())),
            preferred_element_type=F32) * scale
        cell = lane + h * BLOCK
        hit = jnp.sum(jnp.where(q == cell, s, 0.0), axis=1, keepdims=True)
        own_scores.append((s, hit))
        ok = jnp.concatenate(
            [jnp.full((BLOCK, BLOCK), alive(7 + h, r).astype(jnp.int32), jnp.int32) for r in range(2)], 0) > 0
        scores[7 + h] = jnp.where(ok & (half != cell), s, NEG)
    buf[pl.ds(pl.multiple_of((16 + 4 * g) * CHUNK, 4 * CHUNK), n), :] = e_ref[...]
    pos_score[...] = own_scores[0][1] + own_scores[1][1]
    m = jnp.maximum(jnp.max(scores[7], axis=1, keepdims=True), jnp.max(scores[8], axis=1, keepdims=True))
    top[...] = m
    total[...] = jnp.sum(jnp.exp(scores[7] - m), axis=1, keepdims=True) + jnp.sum(
        jnp.exp(scores[8] - m), axis=1, keepdims=True)

    def process(block):
        k = block - (2 * g + 1)

        @pl.when((k >= 0) & (k < 16))
        def _():
            far = buf[pl.ds(pl.multiple_of(block * BLOCK, BLOCK), BLOCK), :]
            for r in range(2):
                part = pl.ds(r * BLOCK, BLOCK)
                s = lax.dot_general(
                    e_ref[part, :], far, (((1,), (1,)), ((), ())),
                    preferred_element_type=F32) * scale
                s = jnp.where(alive(k, r), s, NEG)
                scores[k, part, :] = s
                old = top[part, :]
                new = jnp.maximum(old, jnp.max(s, axis=1, keepdims=True))
                total[part, :] = total[part, :] * jnp.exp(old - new) + jnp.sum(
                    jnp.exp(s - new), axis=1, keepdims=True)
                top[part, :] = new

    def give(slot, also=True):
        when(c_gives(slot) & also, lambda: c_relay(slot).start())

    def event(kind, i):
        if kind == "X":
            slot = oth + 4 * g + i
            arrived(slot)
            when(z_send & z_need(4 * g + i), lambda: z_relay(4 * g + i).start())
            if i >= 2:
                y_relay(i).start()
                y_own(i).start()
            give(slot)
        elif kind == "Y":
            slot = 16 + 4 * gy + i
            arrived(slot)
            if i < 2:
                x_relay(i).start()
                x_own(i).start()
            give(slot)
        elif kind == "D":
            slot = oth + 4 * gy + i
            arrived(slot)
            when(z_gives(i), lambda: z_relay(4 * gy + i).start())
            give(slot)
        else:
            e = 4 * (g if kind == "Z" else gy) + i

            def take():
                arrived(adj + e)
                if kind == "Z" and i >= 2:
                    when(zy_send, lambda: zy_relay(i).start())
                give(adj + e)
            when(z_recv & z_need(e), take)

    def c_wait(block, cond):
        for i in range(2):
            when(c_takes(2 * block + i) & cond, lambda: arrived(2 * block + i))

    def at_block(base, element, h):
        return base // 2 + 2 * element + h

    here = jnp.int32(16)
    steps = [
        ([("X", 2), ("Y", 0)], [(at_block(here, gp, 0), True), (at_block(here, gp, 1), True)]),
        ([("X", 3), ("Y", 1), ("Z", 2)], [(at_block(oth, g, 1), None), (at_block(here, gy, 0), None)]),
        ([("D", 0), ("D", 2), ("Z", 3)], [(at_block(oth, gp, 1), True), (at_block(here, gpy, 0), True)]),
        ([("X", 0), ("Y", 2), ("W", 0)], [(at_block(adj, g, 1), None), (at_block(adj, gp, 1), z_recv)]),
        ([("D", 1), ("D", 3), ("W", 2)], [(at_block(oth, gy, 0), None), (at_block(oth, gy, 1), None)]),
        ([("X", 1), ("Y", 3), ("Z", 0)], [(at_block(oth, g, 0), None), (at_block(here, gy, 1), None)]),
        ([("W", 1)], [(at_block(oth, gp, 0), True), (at_block(here, gpy, 1), True)]),
        ([("W", 3)], [(at_block(oth, gpy, 0), True), (at_block(oth, gpy, 1), True)]),
        ([], [(at_block(adj, gy, 0), None), (at_block(adj, gy, 1), None)]),
        ([], [(at_block(adj, gpy, 0), z_recv), (at_block(adj, gpy, 1), z_recv)]),
        ([("Z", 1)], [(at_block(adj, g, 0), None), (at_block(adj, gp, 0), z_recv)]),
    ]

    def step(u, carry):
        spots = [jnp.int32(0), jnp.int32(0)]
        for index, (events, ready) in enumerate(steps):
            for h in range(2):
                spots[h] = spots[h] + jnp.where(u == index, ready[h][0], 0)

            @pl.when(u == index)
            def _():
                for kind, i in events:
                    event(kind, i)
                for block, cond in ready:
                    if cond is not None:
                        c_wait(block, cond)
        for h in range(2):
            process(spots[h])
        return carry

    lax.fori_loop(0, len(steps), step, 0)

    lse = top[...] + jnp.log(total[...])
    lse_col[...] = lse
    loss = lse - pos_score[...]
    both = jnp.where(
        lax.broadcasted_iota(jnp.int32, (n, 128), 1) < 8,
        jnp.broadcast_to(lse, (n, 128)), jnp.broadcast_to(loss, (n, 128)))
    turned = both.T
    lse_send[...] = turned[:8, :]
    lse_far[4] = turned[:8, :]
    loss_ref[...] = turned[8:9, :]

    def lse_copy(offset):
        return pltpu.make_async_remote_copy(
            src_ref=lse_send, dst_ref=lse_far.at[4 - offset],
            send_sem=ls.at[4 + offset], recv_sem=lr.at[4 - offset],
            device_id=at(me + offset), device_id_type=pl.DeviceIdType.MESH,
        )

    for offset in (-4, 4, -3, 3, -2, 2, -1, 1):
        when(exists(me + offset), lambda: lse_copy(offset).start())

    def fill(k):
        offset = (k - 7) // 2
        h = (k - 7) % 2
        s = scores[k]
        w = jnp.exp(s - lse_col[...]) + jnp.exp(
            s - lse_far[offset + 4][0:1, h * BLOCK:(h + 1) * BLOCK])
        if offset == 0:
            cell = lax.broadcasted_iota(jnp.int32, (n, BLOCK), 1) + h * BLOCK
            line = lax.broadcasted_iota(jnp.int32, (n, BLOCK), 0)
            w = w - (qcol_ref[...] == cell).astype(F32)
            w = w - (qrow_ref[0:1, h * BLOCK:(h + 1) * BLOCK] == line).astype(F32)
        weights[:, k * BLOCK:(k + 1) * BLOCK] = w.astype(jnp.bfloat16)

    fill(7)
    fill(8)
    for offset in (-1, 1, -2, 2, -3, 3, -4, 4):
        when(exists(me + offset), lambda: lse_copy(-offset).wait_recv())
        for k in range(16):
            if (k - 7) // 2 == offset:
                fill(k)

    width = e_ref.shape[1]

    def product(t, carry):
        columns = pl.ds(pl.multiple_of(t * 256, 256), 256)
        near = buf[pl.ds(pl.multiple_of((2 * g + 1) * BLOCK, BLOCK), 16 * BLOCK), columns]
        grad_ref[:, columns] = jnp.dot(weights[...], near, preferred_element_type=F32) * scale
        return carry

    lax.fori_loop(0, width // 256, product, 0)

    for offset in (-4, 4, -3, 3, -2, 2, -1, 1):
        when(exists(me + offset), lambda: lse_copy(offset).wait_send())
    for i in range(4):
        x_own(i).wait_send()
        y_own(i).wait_send()
        c_own(i).wait_send()
        when(z_send & z_need(4 * g + i), lambda: z_relay(4 * g + i).wait_send())
        when(z_gives(i), lambda: z_relay(4 * gy + i).wait_send())
        for slot in (oth + 4 * g + i, 16 + 4 * gy + i, oth + 4 * gy + i):
            when(c_gives(slot), lambda: c_relay(slot).wait_send())
        for e in (4 * g + i, 4 * gy + i):
            when(c_gives(adj + e) & z_recv & z_need(e), lambda: c_relay(adj + e).wait_send())
        if i < 2:
            x_relay(i).wait_send()
        else:
            y_relay(i).wait_send()
            when(zy_send, lambda: zy_relay(i).wait_send())


def solution(mesh):
    row_axis, col_axis = mesh.axis_names
    devices = mesh.shape[row_axis] * mesh.shape[col_axis]
    cols = mesh.shape[col_axis]

    def shards(embeddings, block_cluster, partner_shift):
        rows, width = embeddings.shape
        vmem = pl.BlockSpec(memory_space=pltpu.VMEM)
        grad, loss = pl.pallas_call(
            functools.partial(kernel, row_axis, col_axis, devices, cols, width ** (-0.5)),
            out_shape=(
                jax.ShapeDtypeStruct((rows, width), F32),
                jax.ShapeDtypeStruct((1, rows), F32),
            ),
            in_specs=[pl.BlockSpec(memory_space=pltpu.SMEM), vmem, vmem],
            out_specs=(vmem, vmem),
            scratch_shapes=[
                pltpu.VMEM((24 * BLOCK, width), jnp.bfloat16),
                pltpu.VMEM((16, rows, BLOCK), F32),
                pltpu.VMEM((rows, 16 * BLOCK), jnp.bfloat16),
                pltpu.VMEM((rows, 1), F32),
                pltpu.VMEM((rows, 1), F32),
                pltpu.VMEM((rows, 1), F32),
                pltpu.VMEM((8, rows), F32),
                pltpu.VMEM((2 * REACH + 1, 8, rows), F32),
                pltpu.VMEM((rows, 1), F32),
                pltpu.VMEM((rows, 1), jnp.int32),
                pltpu.VMEM((1, rows), jnp.int32),
                pltpu.SemaphoreType.DMA((48,)),
                pltpu.SemaphoreType.DMA((6,)),
                pltpu.SemaphoreType.DMA((8,)),
                pltpu.SemaphoreType.DMA((48,)),
                pltpu.SemaphoreType.DMA((16,)),
                pltpu.SemaphoreType.DMA((2 * REACH + 1,)),
                pltpu.SemaphoreType.DMA((2 * REACH + 1,)),
            ],
            compiler_params=pltpu.CompilerParams(
                collective_id=0, has_side_effects=True, vmem_limit_bytes=34 * 1024 * 1024
            ),
        )(block_cluster, embeddings, partner_shift.reshape(1, rows))
        return loss.reshape(rows), grad

    in_specs = (P((row_axis, col_axis), None), P(), P((row_axis, col_axis)))
    out_specs = (P((row_axis, col_axis)), P((row_axis, col_axis), None))
    return jax.shard_map(shards, mesh=mesh, in_specs=in_specs, out_specs=out_specs, check_vma=False)
```

```python
import functools

import jax
import jax.numpy as jnp
from jax import lax
from jax.experimental import pallas as pl
from jax.experimental.pallas import tpu as pltpu
from jax.sharding import PartitionSpec as P

BLOCK = 256
REACH = 4
CHUNK = 128
NEG = -1e30
F32 = jnp.float32


def kernel(
    row_axis, col_axis, devices, cols, scale,
    cluster_ref, e_ref, shift_ref,
    grad_ref, loss_ref,
    buf, scores, weights, top, total, lse_col, lse_send, lse_far, pos_score, qcol_ref, qrow_ref,
    recv, xs, ys, cs, zs, ls, lr,
):
    me = lax.axis_index(row_axis) * cols + lax.axis_index(col_axis)
    y = me % 2
    c = me // 2 % 2
    x = me // 4 % 2
    g = 2 * c + y
    gy = 2 * c + 1 - y
    gp = 2 * (1 - c) + y
    gpy = 2 * (1 - c) + 1 - y
    oth = 32 * (1 - x)
    adj = 32 * x
    xpeer = me + 4 - 8 * x
    ypeer = me + 1 - 2 * y
    cpeer = me + 2 - 4 * c
    zto = me + 8 - 16 * x
    zfrom = me - 8 + 16 * x
    z_send = (zto >= 0) & (zto < devices)
    z_recv = (zfrom >= 0) & (zfrom < devices)

    def at(device):
        return (device // cols, device % cols)

    def exists(device):
        return (device >= 0) & (device < devices)

    barrier = pltpu.get_barrier_semaphore()
    count = jnp.int32(0)
    for offset in (-8, -4, -3, -2, -1, 1, 2, 3, 4, 8):
        there = exists(me + offset)
        count = count + there.astype(jnp.int32)

        @pl.when(there)
        def _():
            pl.semaphore_signal(
                barrier, inc=1, device_id=at(me + offset), device_id_type=pl.DeviceIdType.MESH
            )
    pl.semaphore_wait(barrier, count)

    def rows(slot):
        return buf.at[pl.ds(pl.multiple_of(slot * CHUNK, CHUNK), CHUNK), :]

    def remote(src, slot, send, device):
        return pltpu.make_async_remote_copy(
            src_ref=src, dst_ref=rows(slot), send_sem=send, recv_sem=recv.at[slot],
            device_id=at(device), device_id_type=pl.DeviceIdType.MESH,
        )

    def own(i):
        return e_ref.at[pl.ds(i * CHUNK, CHUNK), :]

    def x_own(i):
        return remote(own(i), adj + 4 * g + i, xs.at[i], xpeer)

    def y_own(i):
        return remote(own(i), 16 + 4 * g + i, ys.at[i], ypeer)

    def c_own(i):
        return remote(own(i), 16 + 4 * g + i, cs.at[16 + 4 * g + i], cpeer)

    def x_relay(i):
        return remote(rows(16 + 4 * gy + i), adj + 4 * gy + i, xs.at[4 + i], xpeer)

    def y_relay(i):
        return remote(rows(oth + 4 * g + i), oth + 4 * g + i, ys.at[2 + i], ypeer)

    def z_need(r):
        return jnp.where(x == 0, r >= 4 * y + 2, r <= 4 * y + 9)

    def z_relay(r):
        return remote(rows(oth + r), adj + r, zs.at[r], zto)

    zy_send = z_recv & (c == 0) & (y == 1 - x)
    zy_skip = (c == 0) & (y == x)

    def z_gives(i):
        need = z_send & z_need(4 * gy + i)
        return need & ~zy_skip if i >= 2 else need

    def zy_relay(i):
        return remote(rows(adj + 4 * g + i), adj + 4 * g + i, ys.at[4 + i], ypeer)

    def c_relay(slot):
        return remote(rows(slot), slot, cs.at[slot], cpeer)

    def c_gives(slot):
        return (slot >= 4 * gp + 2) & (slot <= 4 * gp + 33)

    def c_takes(slot):
        return (slot >= 4 * g + 2) & (slot <= 4 * g + 33)

    def arrived(slot):
        remote(rows(slot), slot, zs.at[0], cpeer).wait_recv()

    def when(cond, action):
        pl.when(cond)(action)

    for i in range(2):
        x_own(2 + i).start()
        y_own(i).start()
    for i in range(4):
        c_own(i).start()

    when(~z_recv, lambda: buf.__setitem__(
        (pl.ds(pl.multiple_of(adj * CHUNK, CHUNK), 16 * CHUNK), slice(None)),
        jnp.zeros((16 * CHUNK, buf.shape[1]), buf.dtype)))
    for offset in (-4, -3, -2, -1, 1, 2, 3, 4):
        when(~exists(me + offset), lambda: lse_far.__setitem__(
            offset + 4, jnp.zeros(lse_far.shape[1:], F32)))

    n = e_ref.shape[0]
    blocks = cluster_ref.shape[0]

    def alive(k, r):
        there = 2 * me + k - 7
        near = jnp.maximum(jnp.minimum(there, blocks - 1), 0)
        same = cluster_ref[near] == cluster_ref[2 * me + r]
        return same & (there == near)

    place = lax.broadcasted_iota(jnp.int32, (1, n), 1)
    within = place % BLOCK
    goal = place - within + (within + shift_ref[...]) % BLOCK
    qrow_ref[...] = goal
    qcol_ref[...] = jnp.broadcast_to(goal.astype(F32), (128, n)).T[:, :1].astype(jnp.int32)

    half = lax.broadcasted_iota(jnp.int32, (n, BLOCK), 0)
    lane = lax.broadcasted_iota(jnp.int32, (n, BLOCK), 1)
    q = qcol_ref[...]
    own_scores = []
    for h in range(2):
        s = lax.dot_general(
            e_ref[...], e_ref[h * BLOCK:(h + 1) * BLOCK, :], (((1,), (1,)), ((), ())),
            preferred_element_type=F32) * scale
        cell = lane + h * BLOCK
        hit = jnp.sum(jnp.where(q == cell, s, 0.0), axis=1, keepdims=True)
        own_scores.append((s, hit))
        ok = jnp.concatenate(
            [jnp.full((BLOCK, BLOCK), alive(7 + h, r).astype(jnp.int32), jnp.int32) for r in range(2)], 0) > 0
        scores[7 + h] = jnp.where(ok & (half != cell), s, NEG)
    buf[pl.ds(pl.multiple_of((16 + 4 * g) * CHUNK, 4 * CHUNK), n), :] = e_ref[...]
    pos_score[...] = own_scores[0][1] + own_scores[1][1]
    m = jnp.maximum(jnp.max(scores[7], axis=1, keepdims=True), jnp.max(scores[8], axis=1, keepdims=True))
    top[...] = m
    total[...] = jnp.sum(jnp.exp(scores[7] - m), axis=1, keepdims=True) + jnp.sum(
        jnp.exp(scores[8] - m), axis=1, keepdims=True)

    def process(block):
        k = block - (2 * g + 1)

        @pl.when((k >= 0) & (k < 16))
        def _():
            far = buf[pl.ds(pl.multiple_of(block * BLOCK, BLOCK), BLOCK), :]
            for r in range(2):
                part = pl.ds(r * BLOCK, BLOCK)
                s = lax.dot_general(
                    e_ref[part, :], far, (((1,), (1,)), ((), ())),
                    preferred_element_type=F32) * scale
                s = jnp.where(alive(k, r), s, NEG)
                scores[k, part, :] = s
                old = top[part, :]
                new = jnp.maximum(old, jnp.max(s, axis=1, keepdims=True))
                total[part, :] = total[part, :] * jnp.exp(old - new) + jnp.sum(
                    jnp.exp(s - new), axis=1, keepdims=True)
                top[part, :] = new

    def give(slot, also=True):
        when(c_gives(slot) & also, lambda: c_relay(slot).start())

    def event(kind, i):
        if kind == "X":
            slot = oth + 4 * g + i
            arrived(slot)
            when(z_send & z_need(4 * g + i), lambda: z_relay(4 * g + i).start())
            if i >= 2:
                y_relay(i).start()
                y_own(i).start()
            give(slot)
        elif kind == "Y":
            slot = 16 + 4 * gy + i
            arrived(slot)
            if i < 2:
                x_relay(i).start()
                x_own(i).start()
            give(slot)
        elif kind == "D":
            slot = oth + 4 * gy + i
            arrived(slot)
            when(z_gives(i), lambda: z_relay(4 * gy + i).start())
            give(slot)
        else:
            e = 4 * (g if kind == "Z" else gy) + i

            def take():
                arrived(adj + e)
                if kind == "Z" and i >= 2:
                    when(zy_send, lambda: zy_relay(i).start())
                give(adj + e)
            when(z_recv & z_need(e), take)

    def c_wait(block, cond):
        for i in range(2):
            when(c_takes(2 * block + i) & cond, lambda: arrived(2 * block + i))

    def at_block(base, element, h):
        return base // 2 + 2 * element + h

    here = jnp.int32(16)
    steps = [
        ([("X", 2), ("Y", 0)], [(at_block(here, gp, 0), True), (at_block(here, gp, 1), True)]),
        ([("X", 3), ("Y", 1), ("Z", 2)], [(at_block(oth, g, 1), None), (at_block(here, gy, 0), None)]),
        ([("D", 0), ("D", 2), ("Z", 3)], [(at_block(oth, gp, 1), True), (at_block(here, gpy, 0), True)]),
        ([("X", 0), ("Y", 2), ("W", 0)], [(at_block(adj, g, 1), None), (at_block(adj, gp, 1), z_recv)]),
        ([("D", 1), ("D", 3), ("W", 2)], [(at_block(oth, gy, 0), None), (at_block(oth, gy, 1), None)]),
        ([("X", 1), ("Y", 3), ("Z", 0)], [(at_block(oth, g, 0), None), (at_block(here, gy, 1), None)]),
        ([("W", 1)], [(at_block(oth, gp, 0), True), (at_block(here, gpy, 1), True)]),
        ([("W", 3)], [(at_block(oth, gpy, 0), True), (at_block(oth, gpy, 1), True)]),
        ([], [(at_block(adj, gy, 0), None), (at_block(adj, gy, 1), None)]),
        ([], [(at_block(adj, gpy, 0), z_recv), (at_block(adj, gpy, 1), z_recv)]),
        ([("Z", 1)], [(at_block(adj, g, 0), None), (at_block(adj, gp, 0), z_recv)]),
    ]

    def step(u, carry):
        spots = [jnp.int32(0), jnp.int32(0)]
        for index, (events, ready) in enumerate(steps):
            for h in range(2):
                spots[h] = spots[h] + jnp.where(u == index, ready[h][0], 0)

            @pl.when(u == index)
            def _():
                for kind, i in events:
                    event(kind, i)
                for block, cond in ready:
                    if cond is not None:
                        c_wait(block, cond)
        for h in range(2):
            process(spots[h])
        return carry

    lax.fori_loop(0, len(steps), step, 0)

    lse = top[...] + jnp.log(total[...])
    lse_col[...] = lse
    loss = lse - pos_score[...]
    both = jnp.where(
        lax.broadcasted_iota(jnp.int32, (n, 128), 1) < 8,
        jnp.broadcast_to(lse, (n, 128)), jnp.broadcast_to(loss, (n, 128)))
    turned = both.T
    lse_send[...] = turned[:8, :]
    lse_far[4] = turned[:8, :]
    loss_ref[...] = turned[8]

    def lse_copy(offset):
        return pltpu.make_async_remote_copy(
            src_ref=lse_send, dst_ref=lse_far.at[4 - offset],
            send_sem=ls.at[4 + offset], recv_sem=lr.at[4 - offset],
            device_id=at(me + offset), device_id_type=pl.DeviceIdType.MESH,
        )

    for offset in (-4, 4, -3, 3, -2, 2, -1, 1):
        when(exists(me + offset), lambda: lse_copy(offset).start())

    def fill(k):
        offset = (k - 7) // 2
        h = (k - 7) % 2
        s = scores[k]
        w = jnp.exp(s - lse_col[...]) + jnp.exp(
            s - lse_far[offset + 4][0:1, h * BLOCK:(h + 1) * BLOCK])
        if offset == 0:
            cell = lax.broadcasted_iota(jnp.int32, (n, BLOCK), 1) + h * BLOCK
            line = lax.broadcasted_iota(jnp.int32, (n, BLOCK), 0)
            w = w - (qcol_ref[...] == cell).astype(F32)
            w = w - (qrow_ref[0:1, h * BLOCK:(h + 1) * BLOCK] == line).astype(F32)
        weights[:, k * BLOCK:(k + 1) * BLOCK] = w.astype(jnp.bfloat16)

    width = e_ref.shape[1]

    def part_of(first, many, columns):
        near = buf[pl.ds(pl.multiple_of((2 * g + 1 + first) * BLOCK, BLOCK), many * BLOCK), columns]
        left = weights[:, first * BLOCK:(first + many) * BLOCK]
        return jnp.dot(left, near, preferred_element_type=F32)

    def own_product(t, carry):
        columns = pl.ds(pl.multiple_of(t * 256, 256), 256)
        grad_ref[:, columns] = part_of(7, 2, columns)
        return carry

    def rest_product(t, carry):
        columns = pl.ds(pl.multiple_of(t * 256, 256), 256)
        rest = part_of(0, 7, columns) + part_of(9, 7, columns)
        grad_ref[:, columns] = (grad_ref[:, columns] + rest) * scale
        return carry

    fill(7)
    fill(8)
    lax.fori_loop(0, width // 256, own_product, 0)
    for offset in (-1, 1, -2, 2, -3, 3, -4, 4):
        when(exists(me + offset), lambda: lse_copy(-offset).wait_recv())
        for k in range(16):
            if (k - 7) // 2 == offset:
                fill(k)
    lax.fori_loop(0, width // 256, rest_product, 0)

    for offset in (-4, 4, -3, 3, -2, 2, -1, 1):
        when(exists(me + offset), lambda: lse_copy(offset).wait_send())
    for i in range(4):
        x_own(i).wait_send()
        y_own(i).wait_send()
        c_own(i).wait_send()
        when(z_send & z_need(4 * g + i), lambda: z_relay(4 * g + i).wait_send())
        when(z_gives(i), lambda: z_relay(4 * gy + i).wait_send())
        for slot in (oth + 4 * g + i, 16 + 4 * gy + i, oth + 4 * gy + i):
            when(c_gives(slot), lambda: c_relay(slot).wait_send())
        for e in (4 * g + i, 4 * gy + i):
            when(c_gives(adj + e) & z_recv & z_need(e), lambda: c_relay(adj + e).wait_send())
        if i < 2:
            x_relay(i).wait_send()
        else:
            y_relay(i).wait_send()
            when(zy_send, lambda: zy_relay(i).wait_send())


def solution(mesh):
    row_axis, col_axis = mesh.axis_names
    devices = mesh.shape[row_axis] * mesh.shape[col_axis]
    cols = mesh.shape[col_axis]

    def shards(embeddings, block_cluster, partner_shift):
        rows, width = embeddings.shape
        vmem = pl.BlockSpec(memory_space=pltpu.VMEM)
        grad, loss = pl.pallas_call(
            functools.partial(kernel, row_axis, col_axis, devices, cols, width ** (-0.5)),
            out_shape=(
                jax.ShapeDtypeStruct((rows, width), F32),
                jax.ShapeDtypeStruct((rows,), F32),
            ),
            in_specs=[pl.BlockSpec(memory_space=pltpu.SMEM), vmem, vmem],
            out_specs=(vmem, vmem),
            scratch_shapes=[
                pltpu.VMEM((24 * BLOCK, width), jnp.bfloat16),
                pltpu.VMEM((16, rows, BLOCK), F32),
                pltpu.VMEM((rows, 16 * BLOCK), jnp.bfloat16),
                pltpu.VMEM((rows, 1), F32),
                pltpu.VMEM((rows, 1), F32),
                pltpu.VMEM((rows, 1), F32),
                pltpu.VMEM((8, rows), F32),
                pltpu.VMEM((2 * REACH + 1, 8, rows), F32),
                pltpu.VMEM((rows, 1), F32),
                pltpu.VMEM((rows, 1), jnp.int32),
                pltpu.VMEM((1, rows), jnp.int32),
                pltpu.SemaphoreType.DMA((48,)),
                pltpu.SemaphoreType.DMA((6,)),
                pltpu.SemaphoreType.DMA((8,)),
                pltpu.SemaphoreType.DMA((48,)),
                pltpu.SemaphoreType.DMA((16,)),
                pltpu.SemaphoreType.DMA((2 * REACH + 1,)),
                pltpu.SemaphoreType.DMA((2 * REACH + 1,)),
            ],
            compiler_params=pltpu.CompilerParams(
                collective_id=0, has_side_effects=True, vmem_limit_bytes=34 * 1024 * 1024
            ),
        )(block_cluster, embeddings, partner_shift.reshape(1, rows))
        return loss, grad

    in_specs = (P((row_axis, col_axis), None), P(), P((row_axis, col_axis)))
    out_specs = (P((row_axis, col_axis)), P((row_axis, col_axis), None))
    return jax.shard_map(shards, mesh=mesh, in_specs=in_specs, out_specs=out_specs, check_vma=False)
```
